256 devices in a mesh: gx: 16 (over x, z_hi), gy: 8 (over y, core), ga: 2 (over z_lo).
Axes of the slice: x: 4, y: 4, z: 8 (z_hi: 4, z_lo: 2; z = z_hi * 2 + z_lo), core: 2. Of those that a mesh axis runs over, the one named last changes fastest.
Arguments:
- head: float32 [16, 256, 8192], P(None, 'gx', ('gy', 'ga')), may hold values from -6 to 6
- conductivity: float32 [16, 256, 8192], P(None, 'gx', ('gy', 'ga')), may hold values from 0.1 to 10
- root_layer: int32 [256, 8192], P('gx', ('gy', 'ga')), may hold values from 0 to 15
- veg_type: int32 [256, 8192], P('gx', ('gy', 'ga')), may hold values from 0 to 16
- uptake_rate: float32 [17], replicated, may hold values from 0.2 to 2
- depth: float32 [256, 8192], P('gx'), may hold values from 0.05 to 2
- conveyance: float32 [256, 8192], P('gx'), may hold values from 0.2 to 5
- elevation: float32 [256, 8192], P('gx'), may hold values from -3 to 3
- land_mask: int32 [256, 8192], P('gx'), may hold values 0 or 1
Outputs:
- new_head: float32 [16, 256, 8192], P(None, 'gx', ('gy', 'ga'))
- new_depth: float32 [256, 8192], P('gx')
The draws below stay inside these ranges and needn't reach their ends.
All inputs are finite; a program needn't handle non-finite values. No bound on the sum of `land_mask` on one device may be relied on, other than what follows from the above.
Results may differ from the reference program's by a relative error of at most 0.0003.
Values sent between devices are 32-bit elements; how exact they have to be, the bound alone decides.
A program may use at most 64 MiB of HBM per device.

```python
import math
import jax
import jax.numpy as jnp

L = 16
NVEG = 17
SWEEPS = 2
SSW = 4
NX = 256
NY = 8192


def place_ends(values, rng, low, high):
    dims = values.shape
    index_at = [jax.random.randint(jax.random.fold_in(rng, axis), (), 0, dims[axis]) for axis in range(len(dims))]
    values = values.at[tuple(index_at)].set(low)
    longest = dims.index(max(dims))
    index_at[longest] = (index_at[longest] + 1) % dims[longest]
    return values.at[tuple(index_at)].set(high)


def level_of(own_key, dims, cuts, smallest, high):
    def one(position, shards_of):
        draws = jax.random.uniform(jax.random.fold_in(jax.random.fold_in(own_key, 6), position), (shards_of,), jnp.float32, smallest / len(cuts), high / len(cuts))
        return jnp.repeat(jnp.exp(draws), dims[position] // shards_of).reshape((-1,) + (1,) * (len(dims) - position - 1))

    gain = one(*cuts[0])
    for cut in cuts[1:]:
        gain = gain * one(*cut)
    return gain


def bell_draw(key, dims, width, bound, shards=(), kind=jnp.bfloat16):
    level = level_of(key, dims, shards, -0.22, 0.18) if shards else 1.0
    entries = jax.random.normal(key, dims, jnp.float32) * width * level
    return jnp.minimum(jnp.maximum(entries, -bound), bound).astype(kind)


def setup_inputs(seed: int = 0) -> dict:
    streams_of = jax.random.split(jax.random.key(seed), 10)
    head = bell_draw(streams_of[0], (L, NX, NY), 1.0, 6.0, ((1, 16), (2, 16)), jnp.float32)
    conductivity = jnp.clip(jnp.exp(math.log(10.0) - 4.6051702 * jax.random.uniform(streams_of[1], (L, NX, NY), jnp.float32) ** level_of(streams_of[1], (L, NX, NY), ((1, 16), (2, 16)), -0.2, 0.2)), 0.1, 10.0)
    root_layer = place_ends(jax.random.randint(streams_of[2], (NX, NY), 0, L), jax.random.fold_in(streams_of[2], 1), 0, L - 1).astype(jnp.int32)
    veg_type = place_ends(jax.random.randint(streams_of[3], (NX, NY), 0, NVEG), jax.random.fold_in(streams_of[3], 1), 0, NVEG - 1).astype(jnp.int32)
    uptake_rate = jnp.clip(jnp.exp(jax.random.uniform(streams_of[4], (NVEG,), jnp.float32, math.log(0.2), math.log(2.0))), 0.2, 2.0)
    depth = jnp.clip(jnp.exp(math.log(2.0) - 3.6888794 * jax.random.uniform(streams_of[5], (NX, NY), jnp.float32) ** level_of(streams_of[5], (NX, NY), ((0, 16),), -0.2, 0.2)), 0.05, 2.0)
    conveyance = jnp.clip(jnp.exp(math.log(5.0) - 3.218876 * jax.random.uniform(streams_of[6], (NX, NY), jnp.float32) ** level_of(streams_of[6], (NX, NY), ((0, 16),), -0.2, 0.2)), 0.2, 5.0)
    elevation = bell_draw(streams_of[7], (NX, NY), 0.5, 3.0, ((0, 16),), jnp.float32)
    land_mask = place_ends((jax.random.randint(streams_of[8], (NX, NY), 0, 4) < 3).astype(jnp.int32), jax.random.fold_in(streams_of[8], 1), 0, 1)
    return dict(head=head, conductivity=conductivity, root_layer=root_layer, veg_type=veg_type, uptake_rate=uptake_rate, depth=depth, conveyance=conveyance, elevation=elevation, land_mask=land_mask)


exchange_coef = 0.5
storage_coef = 0.5


def harmonic(first, second):
    total = first + second
    return 2.0 * first * second / jnp.where(total > 0, total, 1.0)


def lateral(field_ext, coef_ext):
    center = coef_ext[..., 1:-1, 1:-1]
    wsum = jnp.zeros_like(center)
    nsum = jnp.zeros_like(center)
    for rows, cols in ((slice(2, None), slice(1, -1)), (slice(None, -2), slice(1, -1)), (slice(1, -1), slice(2, None)), (slice(1, -1), slice(None, -2))):
        weight = harmonic(center, coef_ext[..., rows, cols])
        wsum = wsum + weight
        nsum = nsum + weight * field_ext[..., rows, cols]
    return wsum, nsum


def guarded(numer, denom):
    return jnp.where(denom > 0, numer / jnp.where(denom > 0, denom, 1.0), 0.0)


def surface_sweep(depth_ext, drag_ext, bed_ext, base, diag):
    wsum, nsum = lateral(depth_ext + bed_ext, drag_ext)
    bed = bed_ext[1:-1, 1:-1]
    return guarded(base + nsum - wsum * bed, diag + wsum)


def soil_sweep(head_ext, cond_ext, base, diag):
    cond = cond_ext[:, 1:-1, 1:-1]
    inner = head_ext[:, 1:-1, 1:-1]
    wsum, nsum = lateral(head_ext, cond_ext)
    vertical = harmonic(cond[:-1], cond[1:])
    blank = jnp.zeros_like(cond[:1])
    down = jnp.concatenate([vertical, blank], axis=0)
    upward = jnp.concatenate([blank, vertical], axis=0)
    below = jnp.concatenate([inner[1:], blank], axis=0)
    above = jnp.concatenate([blank, inner[:-1]], axis=0)
    numer = base + nsum + down * (below - 1.0) + upward * (above + 1.0)
    return guarded(numer, diag + wsum + down + upward)


def reference(head, conductivity, root_layer, veg_type, uptake_rate, depth, conveyance, elevation, land_mask):
    coupling = exchange_coef * land_mask.astype(jnp.float32)
    top = head[0]
    drag = conveyance * jnp.power(depth, 5.0 / 3.0)
    pad_two = ((1, 1), (1, 1))
    drag_ext = jnp.pad(drag, pad_two)
    bed_ext = jnp.pad(elevation, pad_two)
    sbase = depth + coupling * top
    sdiag = 1.0 + coupling
    level = depth
    for sweep in range(SSW):
        level = surface_sweep(jnp.pad(level, pad_two), drag_ext, bed_ext, sbase, sdiag)
    rate = uptake_rate[veg_type]
    layers = jnp.arange(L, dtype=jnp.int32)[:, None, None]
    inside = (layers <= root_layer[None]).astype(jnp.float32)
    sink = rate[None] * inside / (root_layer[None].astype(jnp.float32) + 1.0)
    base = storage_coef * head - sink
    base = base.at[0].add(coupling * level)
    diag = jnp.full(head.shape, storage_coef, jnp.float32)
    diag = diag.at[0].add(coupling)
    pad_three = ((0, 0), (1, 1), (1, 1))
    cond_ext = jnp.pad(conductivity, pad_three)
    current = head
    for sweep in range(SWEEPS):
        current = soil_sweep(jnp.pad(current, pad_three), cond_ext, base, diag)
    return current, level
```

```python
import functools

import jax
import jax.numpy as jnp
from jax import lax
from jax.experimental import pallas as pl
from jax.experimental.pallas import tpu as pltpu
from jax.sharding import PartitionSpec as P

NVEG = 17
SSW = 4
RING = 4
LANES = 128
EDGE = 2 * LANES

exchange_coef = 0.5
storage_coef = 0.5
MESH = pl.DeviceIdType.MESH


def harmonic(first, second):
    total = first + second
    return 2.0 * first * second / jnp.where(total > 0, total, 1.0)


def lane_of(shape):
    return lax.broadcasted_iota(jnp.int32, shape, len(shape) - 1)


def row_of(shape):
    return lax.broadcasted_iota(jnp.int32, shape, len(shape) - 2)


def from_right(x, edge):
    width = x.shape[1]
    y = pltpu.roll(x, width - 1, 1)
    tail = jnp.where(lane_of(edge.shape) == LANES - 1, edge, y[:, width - LANES :])
    return jnp.concatenate([y[:, : width - LANES], tail], axis=1)


def from_left(x, edge):
    y = pltpu.roll(x, 1, 1)
    front = jnp.where(lane_of(edge.shape) == 0, edge, y[:, :LANES])
    return jnp.concatenate([front, y[:, LANES:]], axis=1)


def circular(window, cols):
    left = window[:, :LANES]
    right = window[:, cols + LANES :]
    side = jnp.where(lane_of(left.shape) < LANES // 2, right, left)
    return jnp.concatenate([window[:, LANES : cols + LANES], side], axis=1)


def kernel(
    head, cond, root, veg, uptake, depth, conv, elev, mask,
    new_head, new_depth,
    hx, cx, px, qx, root_v, veg_v, field, mask_v, top_v, level_v, cpl_v, sink_v,
    wr_v, wl_v, wu_v, wv_v, inv_v, base_v,
    pack_s, pack_r, pack2_s, pack2_r,
    load_sem, send_sem, recv_sem, gsend_sem, grecv_sem, out_sem,
):
    layers, rows, cols = head.shape
    gx = lax.axis_index("gx")
    gy = lax.axis_index("gy")
    ga = lax.axis_index("ga")
    ngx = lax.axis_size("gx")
    nga = lax.axis_size("ga")
    ncol = lax.axis_size("gy") * nga
    col = gy * nga + ga
    off = pl.multiple_of(col * cols, LANES)
    total = ncol * cols

    def at(dx, dc):
        c = lax.rem(col + dc + ncol, ncol)
        return (lax.rem(gx + dx + ngx, ngx), c // nga, lax.rem(c, nga))

    left_off = pl.multiple_of(lax.rem(off - LANES + total, total), LANES)
    right_off = pl.multiple_of(lax.rem(off + cols, total), LANES)
    loads = []
    for n, src in enumerate((depth, conv, elev)):
        loads.append(pltpu.make_async_copy(src.at[:, pl.ds(left_off, LANES)], field.at[n, 0:rows, 0:LANES], load_sem.at[3 * n]))
        loads.append(pltpu.make_async_copy(src.at[:, pl.ds(off, cols)], field.at[n, 0:rows, LANES : LANES + cols], load_sem.at[3 * n + 1]))
        loads.append(pltpu.make_async_copy(src.at[:, pl.ds(right_off, LANES)], field.at[n, 0:rows, LANES + cols :], load_sem.at[3 * n + 2]))
    loads.append(pltpu.make_async_copy(mask.at[:, pl.ds(left_off, LANES)], mask_v.at[0:rows, 0:LANES], load_sem.at[9]))
    loads.append(pltpu.make_async_copy(mask.at[:, pl.ds(off, cols)], mask_v.at[0:rows, LANES : LANES + cols], load_sem.at[10]))
    loads.append(pltpu.make_async_copy(mask.at[:, pl.ds(right_off, LANES)], mask_v.at[0:rows, LANES + cols :], load_sem.at[11]))
    loads.append(pltpu.make_async_copy(head.at[0], top_v.at[0:rows, LANES : LANES + cols], load_sem.at[12]))
    loads.append(pltpu.make_async_copy(root, root_v, load_sem.at[13]))
    loads.append(pltpu.make_async_copy(veg, veg_v, load_sem.at[14]))
    for c in loads:
        c.start()
    for r in range(rows):
        pltpu.make_async_copy(head.at[:, r, :], hx.at[r + 1], load_sem.at[15]).start()
        pltpu.make_async_copy(cond.at[:, r, :], cx.at[r + 1], load_sem.at[16]).start()

    barrier = pltpu.get_barrier_semaphore()
    peers = [at(0, d) for d in range(1, ncol)]
    peers += [at(1, 0), at(-1, 0), at(1, 1), at(1, -1), at(-1, 1), at(-1, -1)]
    for peer in peers:
        pl.semaphore_signal(barrier, inc=1, device_id=peer, device_id_type=MESH)
    for c in loads:
        c.wait()
    pl.semaphore_wait(barrier, len(peers))

    sent = []
    count = [0]

    def send(src, dst, device):
        n = count[0]
        count[0] += 1
        c = pltpu.make_async_remote_copy(
            src_ref=src, dst_ref=dst, send_sem=send_sem.at[n], recv_sem=recv_sem.at[n],
            device_id=device, device_id_type=MESH,
        )
        c.start()
        sent.append(c)
        return c

    lo = pl.ds(rows, RING)
    hi = pl.ds(rows + RING, RING)
    first = pl.ds(0, RING)
    last = pl.ds(rows - RING, RING)
    own = pl.ds(LANES, cols)
    lt = pl.ds(0, LANES)
    rt = pl.ds(LANES + cols, LANES)
    hl = pl.ds(0, LANES)
    hr = pl.ds(cols - LANES, LANES)
    surface = [
        send(field.at[:, last, :], field.at[:, hi, :], at(1, 0)),
        send(field.at[:, first, :], field.at[:, lo, :], at(-1, 0)),
        send(mask_v.at[last, :], mask_v.at[hi, :], at(1, 0)),
        send(mask_v.at[first, :], mask_v.at[lo, :], at(-1, 0)),
        send(head.at[0, last, :], top_v.at[hi, own], at(1, 0)),
        send(head.at[0, first, :], top_v.at[lo, own], at(-1, 0)),
        send(head.at[0, last, hr], top_v.at[hi, lt], at(1, 1)),
        send(head.at[0, last, hl], top_v.at[hi, rt], at(1, -1)),
        send(head.at[0, first, hr], top_v.at[lo, lt], at(-1, 1)),
        send(head.at[0, first, hl], top_v.at[lo, rt], at(-1, -1)),
        send(head.at[0, :, hr], top_v.at[pl.ds(0, rows), lt], at(0, 1)),
        send(head.at[0, :, hl], top_v.at[pl.ds(0, rows), rt], at(0, -1)),
    ]

    pltpu.make_async_copy(hx.at[pl.ds(1, rows)], hx.at[pl.ds(1, rows)], load_sem.at[15]).wait()
    pltpu.make_async_copy(cx.at[pl.ds(1, rows)], cx.at[pl.ds(1, rows)], load_sem.at[16]).wait()
    soil = [
        send(hx.at[rows], hx.at[0], at(1, 0)),
        send(cx.at[rows], cx.at[0], at(1, 0)),
        send(hx.at[1], hx.at[rows + 1], at(-1, 0)),
        send(cx.at[1], cx.at[rows + 1], at(-1, 0)),
    ]

    def pack(fields, out):
        to_right = jnp.zeros((layers, LANES), jnp.float32)
        to_left = jnp.zeros((layers, LANES), jnp.float32)
        lane = lane_of((layers, LANES))
        for n, ref in enumerate(fields):
            for r in range(rows):
                slot = n * rows + r
                tail = pltpu.roll(ref[r + 1, :, cols - LANES : cols], (slot + 1) % LANES, 1)
                to_right = jnp.where(lane == slot, tail, to_right)
                front = ref[r + 1, :, 0:LANES]
                front = pltpu.roll(front, slot, 1) if slot else front
                to_left = jnp.where(lane == slot, front, to_left)
        out[0] = to_right
        out[1] = to_left

    pack((hx, cx), pack_s)
    soil += [
        send(pack_s.at[0], pack_r.at[0], at(0, 1)),
        send(pack_s.at[1], pack_r.at[1], at(0, -1)),
    ]

    rate = jnp.zeros((rows, cols), jnp.float32)
    kinds = veg_v[...]
    for k in range(NVEG):
        rate = jnp.where(kinds == k, uptake[k], rate)
    sink_v[...] = rate / (root_v[...].astype(jnp.float32) + 1.0)

    for c in surface:
        c.wait_recv()
    high = rows + 2 * RING
    wide = cols + LANES
    rowi = row_of((high, wide))
    lane = lane_of((high, wide))
    outside = (rowi >= rows) & (rowi < rows + RING) & (gx == ngx - 1)
    outside |= (rowi >= rows + RING) & (gx == 0)
    outside |= (lane >= cols) & (lane < cols + LANES // 2) & (col == ncol - 1)
    outside |= (lane >= cols + LANES // 2) & (col == 0)
    dep = circular(field[0], cols)
    con = circular(field[1], cols)
    bed = circular(field[2], cols)
    cpl = exchange_coef * circular(mask_v[...], cols).astype(jnp.float32)
    top = circular(top_v[...], cols)
    drag = con * jnp.exp(jnp.log(dep) * (5.0 / 3.0))
    drag = jnp.where(outside, 0.0, drag)
    w_r = harmonic(drag, pltpu.roll(drag, wide - 1, 1))
    w_l = pltpu.roll(w_r, 1, 1)
    w_d = harmonic(drag, pltpu.roll(drag, high - 1, 0))
    w_u = pltpu.roll(w_d, 1, 0)
    wsum = (w_r + w_l) + (w_d + w_u)
    inv = 1.0 / (1.0 + cpl + wsum)
    part = (dep + cpl * top - wsum * bed) * inv
    w_r = w_r * inv
    w_l = w_l * inv
    w_d = w_d * inv
    w_u = w_u * inv
    level = dep
    for _ in range(SSW):
        t = level + bed
        level = part + (
            (w_r * pltpu.roll(t, wide - 1, 1) + w_l * pltpu.roll(t, 1, 1))
            + (w_d * pltpu.roll(t, high - 1, 0) + w_u * pltpu.roll(t, 1, 0))
        )
    block = level[0:rows, 0:cols]
    level_v[...] = block
    coupling = cpl[0:rows, 0:cols]
    cpl_v[0] = coupling
    cpl_v[1] = coupling * block

    gather = []
    for d in range(1, ncol):
        c = pltpu.make_async_remote_copy(
            src_ref=level_v, dst_ref=new_depth.at[:, pl.ds(off, cols)],
            send_sem=gsend_sem.at[d - 1], recv_sem=grecv_sem.at[d - 1],
            device_id=at(0, d), device_id_type=MESH,
        )
        c.start()
        gather.append(c)
    mine = pltpu.make_async_copy(level_v, new_depth.at[:, pl.ds(off, cols)], out_sem.at[0])
    mine.start()

    for c in soil:
        c.wait_recv()
    has_up = jnp.where(gx > 0, 1.0, 0.0)
    has_down = jnp.where(gx < ngx - 1, 1.0, 0.0)
    has_left = jnp.where(col > 0, 1.0, 0.0)
    has_right = jnp.where(col < ncol - 1, 1.0, 0.0)
    layer = row_of((layers, cols))
    lane0 = lane_of((layers, LANES)) == 0

    def right_edge(packed, slot):
        return pltpu.roll(packed, lax.rem(2 * LANES - 1 - slot, LANES), 1)

    def left_edge(packed, slot):
        return pltpu.roll(packed, lax.rem(2 * LANES - slot, LANES), 1)

    def first_sweep(r, w_up):
        c0 = cx[r + 1]
        h0 = hx[r + 1]
        w_down = harmonic(c0, cx[r + 2]) * jnp.where(r == rows - 1, has_down, 1.0)
        edge_r = right_edge(pack_r[1], rows + r) * has_right
        edge_l = left_edge(pack_r[0], rows + r) * has_left
        w_right = harmonic(c0, from_right(c0, edge_r))
        w_left = from_left(w_right, harmonic(c0[:, :LANES], edge_l))
        w_below = jnp.where(layer == layers - 1, 0.0, harmonic(c0, pltpu.roll(c0, layers - 1, 0)))
        w_above = pltpu.roll(w_below, 1, 0)
        on_top = layer == 0
        coupled = jnp.where(on_top, cpl_v[0, pl.ds(r, 1), :], 0.0)
        source = jnp.where(on_top, cpl_v[1, pl.ds(r, 1), :], 0.0)
        uptake_here = jnp.where(layer <= root_v[pl.ds(r, 1), :], sink_v[pl.ds(r, 1), :], 0.0)
        inv_here = 1.0 / (
            (storage_coef + coupled) + ((w_right + w_left) + (w_up + w_down)) + (w_below + w_above)
        )
        base = (storage_coef * h0 - uptake_here + source) + (w_above - w_below)
        wr_v[r] = w_right
        wl_v[r] = w_left
        wu_v[r] = w_up
        wv_v[r] = w_below
        inv_v[r] = inv_here
        base_v[r] = base
        acc = base + w_right * from_right(h0, right_edge(pack_r[1], r)) + w_left * from_left(h0, left_edge(pack_r[0], r))
        acc += w_up * hx[r] + w_down * hx[r + 2]
        acc += w_below * pltpu.roll(h0, layers - 1, 0) + w_above * pltpu.roll(h0, 1, 0)
        px[r + 1] = acc * inv_here
        return w_down

    wu_v[rows] = lax.fori_loop(0, rows, first_sweep, harmonic(cx[0], cx[1]) * has_up)

    second = [
        send(px.at[rows], px.at[0], at(1, 0)),
        send(px.at[1], px.at[rows + 1], at(-1, 0)),
    ]
    pack((px,), pack2_s)
    second += [
        send(pack2_s.at[0], pack2_r.at[0], at(0, 1)),
        send(pack2_s.at[1], pack2_r.at[1], at(0, -1)),
    ]
    for c in second:
        c.wait_recv()

    def second_sweep(r, carry):
        p0 = px[r + 1]
        w_below = wv_v[r]
        w_above = pltpu.roll(w_below, 1, 0)
        acc = base_v[r] + wr_v[r] * from_right(p0, right_edge(pack2_r[1], r)) + wl_v[r] * from_left(p0, left_edge(pack2_r[0], r))
        acc += wu_v[r] * px[r] + wu_v[r + 1] * px[r + 2]
        acc += w_below * pltpu.roll(p0, layers - 1, 0) + w_above * pltpu.roll(p0, 1, 0)
        qx[r] = acc * inv_v[r]
        return carry

    lax.fori_loop(0, rows, second_sweep, 0)
    for r in range(rows):
        pltpu.make_async_copy(qx.at[r], new_head.at[:, r, :], out_sem.at[1]).start()

    for c in sent:
        c.wait_send()
    for c in gather:
        c.wait()
    mine.wait()
    pltpu.make_async_copy(qx, qx, out_sem.at[1]).wait()


def body(head, conductivity, root_layer, veg_type, uptake_rate, depth, conveyance, elevation, land_mask):
    layers, rows, cols = head.shape
    ncol = lax.axis_size("gy") * lax.axis_size("ga")
    f32 = jnp.float32
    slab = (rows, layers, cols)
    ext = (rows + 2, layers, cols)
    hbm = pl.BlockSpec(memory_space=pl.ANY)
    window = (rows + 2 * RING, cols + EDGE)
    return pl.pallas_call(
        kernel,
        out_shape=(
            jax.ShapeDtypeStruct(head.shape, f32),
            jax.ShapeDtypeStruct(depth.shape, f32),
        ),
        in_specs=[hbm] * 4 + [pl.BlockSpec(memory_space=pltpu.SMEM)] + [hbm] * 4,
        out_specs=(hbm, hbm),
        scratch_shapes=[
            pltpu.VMEM(ext, f32),
            pltpu.VMEM(ext, f32),
            pltpu.VMEM(ext, f32),
            pltpu.VMEM(slab, f32),
            pltpu.VMEM((rows, cols), jnp.int32),
            pltpu.VMEM((rows, cols), jnp.int32),
            pltpu.VMEM((3,) + window, f32),
            pltpu.VMEM(window, jnp.int32),
            pltpu.VMEM(window, f32),
            pltpu.VMEM((rows, cols), f32),
            pltpu.VMEM((2, rows, cols), f32),
            pltpu.VMEM((rows, cols), f32),
            pltpu.VMEM(slab, f32),
            pltpu.VMEM(slab, f32),
            pltpu.VMEM((rows + 1, layers, cols), f32),
            pltpu.VMEM(slab, f32),
            pltpu.VMEM(slab, f32),
            pltpu.VMEM(slab, f32),
            pltpu.VMEM((2, layers, LANES), f32),
            pltpu.VMEM((2, layers, LANES), f32),
            pltpu.VMEM((2, layers, LANES), f32),
            pltpu.VMEM((2, layers, LANES), f32),
            pltpu.SemaphoreType.DMA((17,)),
            pltpu.SemaphoreType.DMA((22,)),
            pltpu.SemaphoreType.DMA((22,)),
            pltpu.SemaphoreType.DMA((ncol - 1,)),
            pltpu.SemaphoreType.DMA((ncol - 1,)),
            pltpu.SemaphoreType.DMA((2,)),
        ],
        compiler_params=pltpu.CompilerParams(collective_id=0, has_side_effects=True),
        name="watershed_step",
    )(head, conductivity, root_layer, veg_type, uptake_rate, depth, conveyance, elevation, land_mask)


def solution(mesh):
    return jax.shard_map(
        body,
        mesh=mesh,
        in_specs=(
            P(None, "gx", ("gy", "ga")),
            P(None, "gx", ("gy", "ga")),
            P("gx", ("gy", "ga")),
            P("gx", ("gy", "ga")),
            P(),
            P("gx", None),
            P("gx", None),
            P("gx", None),
            P("gx", None),
        ),
        out_specs=(P(None, "gx", ("gy", "ga")), P("gx", None)),
        check_vma=False,
    )
```

```python
import functools

import jax
import jax.numpy as jnp
from jax import lax
from jax.experimental import pallas as pl
from jax.experimental.pallas import tpu as pltpu
from jax.sharding import PartitionSpec as P

NVEG = 17
SSW = 4
RING = 4
LANES = 128
EDGE = 2 * LANES

exchange_coef = 0.5
storage_coef = 0.5
MESH = pl.DeviceIdType.MESH


def harmonic(first, second):
    total = first + second
    return 2.0 * first * second / jnp.where(total > 0, total, 1.0)


def lane_of(shape):
    return lax.broadcasted_iota(jnp.int32, shape, len(shape) - 1)


def row_of(shape):
    return lax.broadcasted_iota(jnp.int32, shape, len(shape) - 2)


def from_right(x, edge):
    width = x.shape[1]
    y = pltpu.roll(x, width - 1, 1)
    tail = jnp.where(lane_of(edge.shape) == LANES - 1, edge, y[:, width - LANES :])
    return jnp.concatenate([y[:, : width - LANES], tail], axis=1)


def from_left(x, edge):
    y = pltpu.roll(x, 1, 1)
    front = jnp.where(lane_of(edge.shape) == 0, edge, y[:, :LANES])
    return jnp.concatenate([front, y[:, LANES:]], axis=1)


def circular(window, cols):
    left = window[:, :LANES]
    right = window[:, cols + LANES :]
    side = jnp.where(lane_of(left.shape) < LANES // 2, right, left)
    return jnp.concatenate([window[:, LANES : cols + LANES], side], axis=1)


def kernel(
    head, cond, root, veg, uptake, depth, conv, elev, mask,
    new_head, new_depth,
    hx, cx, px, qx, root_v, veg_v, field, mask_v, top_v, cpl_v, sink_v,
    wr_v, wl_v, wu_v, wv_v, inv_v, base_v,
    pack_s, pack_r, pack2_s, pack2_r,
    load_sem, send_sem, recv_sem, gsend_sem, grecv_sem, rsend_sem, rrecv_sem, out_sem,
):
    layers, rows, cols = head.shape
    gx = lax.axis_index("gx")
    gy = lax.axis_index("gy")
    ga = lax.axis_index("ga")
    ngx = lax.axis_size("gx")
    nga = lax.axis_size("ga")
    ncol = lax.axis_size("gy") * nga
    col = gy * nga + ga
    off = pl.multiple_of(col * cols, LANES)
    total = ncol * cols

    def at(dx, dc):
        c = lax.rem(col + dc + ncol, ncol)
        return (lax.rem(gx + dx + ngx, ngx), c // nga, lax.rem(c, nga))

    ngy = lax.axis_size("gy")

    def same_core(dy, dz):
        return (gx, lax.rem(gy + 2 * dy + ngy, ngy), lax.rem(ga + dz + nga, nga))

    def block_cols(device):
        return pl.ds(pl.multiple_of((device[1] * nga + device[2]) * cols, LANES), cols)

    chips = sorted(
        ((dy, dz) for dy in range(ngy // 2) for dz in range(nga) if (dy, dz) != (0, 0)),
        key=lambda v: min(v[0], ngy // 2 - v[0]) + v[1],
    )
    partner = (gx, gy + 1 - 2 * lax.rem(gy, 2), ga)
    barrier = pltpu.get_barrier_semaphore()
    peers = [at(1, 0), at(-1, 0), at(1, 1), at(1, -1), at(-1, 1), at(-1, -1), at(0, 1), at(0, -1), partner]
    peers += [same_core(*v) for v in chips]
    for peer in peers:
        pl.semaphore_signal(barrier, inc=1, device_id=peer, device_id_type=MESH)

    left_off = pl.multiple_of(lax.rem(off - LANES + total, total), LANES)
    right_off = pl.multiple_of(lax.rem(off + cols, total), LANES)
    loads = []
    for n, src in enumerate((depth, conv, elev)):
        loads.append(pltpu.make_async_copy(src.at[:, pl.ds(left_off, LANES)], field.at[n, 0:rows, 0:LANES], load_sem.at[3 * n]))
        loads.append(pltpu.make_async_copy(src.at[:, pl.ds(off, cols)], field.at[n, 0:rows, LANES : LANES + cols], load_sem.at[3 * n + 1]))
        loads.append(pltpu.make_async_copy(src.at[:, pl.ds(right_off, LANES)], field.at[n, 0:rows, LANES + cols :], load_sem.at[3 * n + 2]))
    loads.append(pltpu.make_async_copy(mask.at[:, pl.ds(left_off, LANES)], mask_v.at[0:rows, 0:LANES], load_sem.at[9]))
    loads.append(pltpu.make_async_copy(mask.at[:, pl.ds(off, cols)], mask_v.at[0:rows, LANES : LANES + cols], load_sem.at[10]))
    loads.append(pltpu.make_async_copy(mask.at[:, pl.ds(right_off, LANES)], mask_v.at[0:rows, LANES + cols :], load_sem.at[11]))
    loads.append(pltpu.make_async_copy(head.at[0], top_v.at[0:rows, LANES : LANES + cols], load_sem.at[12]))
    loads.append(pltpu.make_async_copy(root, root_v, load_sem.at[13]))
    loads.append(pltpu.make_async_copy(veg, veg_v, load_sem.at[14]))
    for c in loads:
        c.start()
    for r in range(rows):
        pltpu.make_async_copy(head.at[:, r, :], hx.at[r + 1], load_sem.at[15]).start()
        pltpu.make_async_copy(cond.at[:, r, :], cx.at[r + 1], load_sem.at[16]).start()
    for c in loads:
        c.wait()
    pl.semaphore_wait(barrier, len(peers))

    sent = []
    count = [0]

    def send(src, dst, device):
        n = count[0]
        count[0] += 1
        c = pltpu.make_async_remote_copy(
            src_ref=src, dst_ref=dst, send_sem=send_sem.at[n], recv_sem=recv_sem.at[n],
            device_id=device, device_id_type=MESH,
        )
        c.start()
        sent.append(c)
        return c

    lo = pl.ds(rows, RING)
    hi = pl.ds(rows + RING, RING)
    first = pl.ds(0, RING)
    last = pl.ds(rows - RING, RING)
    own = pl.ds(LANES, cols)
    lt = pl.ds(0, LANES)
    rt = pl.ds(LANES + cols, LANES)
    hl = pl.ds(0, LANES)
    hr = pl.ds(cols - LANES, LANES)
    surface = [
        send(field.at[:, last, :], field.at[:, hi, :], at(1, 0)),
        send(field.at[:, first, :], field.at[:, lo, :], at(-1, 0)),
        send(mask_v.at[last, :], mask_v.at[hi, :], at(1, 0)),
        send(mask_v.at[first, :], mask_v.at[lo, :], at(-1, 0)),
        send(head.at[0, last, :], top_v.at[hi, own], at(1, 0)),
        send(head.at[0, first, :], top_v.at[lo, own], at(-1, 0)),
        send(head.at[0, last, hr], top_v.at[hi, lt], at(1, 1)),
        send(head.at[0, last, hl], top_v.at[hi, rt], at(1, -1)),
        send(head.at[0, first, hr], top_v.at[lo, lt], at(-1, 1)),
        send(head.at[0, first, hl], top_v.at[lo, rt], at(-1, -1)),
        send(head.at[0, :, hr], top_v.at[pl.ds(0, rows), lt], at(0, 1)),
        send(head.at[0, :, hl], top_v.at[pl.ds(0, rows), rt], at(0, -1)),
    ]
    soil = [
        send(head.at[:, rows - 1, :], hx.at[0], at(1, 0)),
        send(cond.at[:, rows - 1, :], cx.at[0], at(1, 0)),
        send(head.at[:, 0, :], hx.at[rows + 1], at(-1, 0)),
        send(cond.at[:, 0, :], cx.at[rows + 1], at(-1, 0)),
    ]

    def surface_block(high, outside):
        wide = cols + LANES
        dep = circular(field[0, 0:high, :], cols)
        con = circular(field[1, 0:high, :], cols)
        bed = circular(field[2, 0:high, :], cols)
        cpl = exchange_coef * circular(mask_v[0:high, :], cols).astype(jnp.float32)
        top = circular(top_v[0:high, :], cols)
        drag = con * jnp.exp(jnp.log(dep) * (5.0 / 3.0))
        lane = lane_of((high, wide))
        outside |= (lane >= cols) & (lane < cols + LANES // 2) & (col == ncol - 1)
        outside |= (lane >= cols + LANES // 2) & (col == 0)
        drag = jnp.where(outside, 0.0, drag)
        w_r = harmonic(drag, pltpu.roll(drag, wide - 1, 1))
        w_l = pltpu.roll(w_r, 1, 1)
        w_d = harmonic(drag, pltpu.roll(drag, high - 1, 0))
        w_u = pltpu.roll(w_d, 1, 0)
        wsum = (w_r + w_l) + (w_d + w_u)
        inv = 1.0 / (1.0 + cpl + wsum)
        part = (dep + cpl * top - wsum * bed) * inv
        w_r = w_r * inv
        w_l = w_l * inv
        w_d = w_d * inv
        w_u = w_u * inv
        level = dep
        for _ in range(SSW):
            t = level + bed
            level = part + (
                (w_r * pltpu.roll(t, wide - 1, 1) + w_l * pltpu.roll(t, 1, 1))
                + (w_d * pltpu.roll(t, high - 1, 0) + w_u * pltpu.roll(t, 1, 0))
            )
        return level, cpl

    def spread():
        mine = block_cols((gx, gy, ga))
        out = []
        for n, device in enumerate([partner] + [same_core(*v) for v in chips]):
            c = pltpu.make_async_remote_copy(
                src_ref=new_depth.at[:, mine], dst_ref=new_depth.at[:, mine],
                send_sem=gsend_sem.at[n], recv_sem=grecv_sem.at[n],
                device_id=device, device_id_type=MESH,
            )
            c.start()
            out.append(c)
        return out

    def relay(n):
        dy, dz = chips[n]
        theirs = block_cols(same_core(-dy, -dz))
        c = pltpu.make_async_remote_copy(
            src_ref=new_depth.at[:, theirs], dst_ref=new_depth.at[:, theirs],
            send_sem=rsend_sem.at[n], recv_sem=rrecv_sem.at[n],
            device_id=partner, device_id_type=MESH,
        )
        c.start()
        return c

    pltpu.make_async_copy(hx.at[pl.ds(1, rows)], hx.at[pl.ds(1, rows)], load_sem.at[15]).wait()
    pltpu.make_async_copy(cx.at[pl.ds(1, rows)], cx.at[pl.ds(1, rows)], load_sem.at[16]).wait()

    def pack(fields, out):
        to_right = jnp.zeros((layers, LANES), jnp.float32)
        to_left = jnp.zeros((layers, LANES), jnp.float32)
        lane = lane_of((layers, LANES))
        for n, ref in enumerate(fields):
            for r in range(rows):
                slot = n * rows + r
                tail = pltpu.roll(ref[r + 1, :, cols - LANES : cols], (slot + 1) % LANES, 1)
                to_right = jnp.where(lane == slot, tail, to_right)
                front = ref[r + 1, :, 0:LANES]
                front = pltpu.roll(front, slot, 1) if slot else front
                to_left = jnp.where(lane == slot, front, to_left)
        out[0] = to_right
        out[1] = to_left

    pack((hx, cx), pack_s)
    soil += [
        send(pack_s.at[0], pack_r.at[0], at(0, 1)),
        send(pack_s.at[1], pack_r.at[1], at(0, -1)),
    ]

    rate = jnp.zeros((rows, cols), jnp.float32)
    kinds = veg_v[...]
    for k in range(NVEG):
        rate = jnp.where(kinds == k, uptake[k], rate)
    sink_v[...] = rate / (root_v[...].astype(jnp.float32) + 1.0)

    for c in surface:
        c.wait_recv()
    high = rows + 2 * RING
    rowi = row_of((high, cols + LANES))
    outside = (rowi >= rows) & (rowi < rows + RING) & (gx == ngx - 1)
    outside |= (rowi >= rows + RING) & (gx == 0)
    level, cpl = surface_block(high, outside)
    block = level[0:rows, 0:cols]
    new_depth[:, block_cols((gx, gy, ga))] = block
    gather = spread()
    coupling = cpl[0:rows, 0:cols]
    cpl_v[0] = coupling
    cpl_v[1] = coupling * block

    for c in soil:
        c.wait_recv()
    has_up = jnp.where(gx > 0, 1.0, 0.0)
    has_down = jnp.where(gx < ngx - 1, 1.0, 0.0)
    has_left = jnp.where(col > 0, 1.0, 0.0)
    has_right = jnp.where(col < ncol - 1, 1.0, 0.0)
    layer = row_of((layers, cols))
    lane0 = lane_of((layers, LANES)) == 0

    def right_edge(packed, slot):
        return pltpu.roll(packed, lax.rem(2 * LANES - 1 - slot, LANES), 1)

    def left_edge(packed, slot):
        return pltpu.roll(packed, lax.rem(2 * LANES - slot, LANES), 1)

    def first_sweep(r, w_up):
        c0 = cx[r + 1]
        h0 = hx[r + 1]
        w_down = harmonic(c0, cx[r + 2]) * jnp.where(r == rows - 1, has_down, 1.0)
        edge_r = right_edge(pack_r[1], rows + r) * has_right
        edge_l = left_edge(pack_r[0], rows + r) * has_left
        w_right = harmonic(c0, from_right(c0, edge_r))
        w_left = from_left(w_right, harmonic(c0[:, :LANES], edge_l))
        w_below = jnp.where(layer == layers - 1, 0.0, harmonic(c0, pltpu.roll(c0, layers - 1, 0)))
        w_above = pltpu.roll(w_below, 1, 0)
        on_top = layer == 0
        coupled = jnp.where(on_top, cpl_v[0, pl.ds(r, 1), :], 0.0)
        source = jnp.where(on_top, cpl_v[1, pl.ds(r, 1), :], 0.0)
        uptake_here = jnp.where(layer <= root_v[pl.ds(r, 1), :], sink_v[pl.ds(r, 1), :], 0.0)
        inv_here = 1.0 / (
            (storage_coef + coupled) + ((w_right + w_left) + (w_up + w_down)) + (w_below + w_above)
        )
        base = (storage_coef * h0 - uptake_here + source) + (w_above - w_below)
        wr_v[r] = w_right
        wl_v[r] = w_left
        wu_v[r] = w_up
        wv_v[r] = w_below
        inv_v[r] = inv_here
        base_v[r] = base
        acc = base + w_right * from_right(h0, right_edge(pack_r[1], r)) + w_left * from_left(h0, left_edge(pack_r[0], r))
        acc += w_up * hx[r] + w_down * hx[r + 2]
        acc += w_below * pltpu.roll(h0, layers - 1, 0) + w_above * pltpu.roll(h0, 1, 0)
        px[r + 1] = acc * inv_here
        return w_down

    wu_v[rows] = lax.fori_loop(0, rows, first_sweep, harmonic(cx[0], cx[1]) * has_up)

    second = [
        send(px.at[rows], px.at[0], at(1, 0)),
        send(px.at[1], px.at[rows + 1], at(-1, 0)),
    ]
    pack((px,), pack2_s)
    second += [
        send(pack2_s.at[0], pack2_r.at[0], at(0, 1)),
        send(pack2_s.at[1], pack2_r.at[1], at(0, -1)),
    ]
    relays = []
    for n in range(len(chips)):
        gather[n + 1].wait_recv()
        relays.append(relay(n))
    for c in second:
        c.wait_recv()

    def second_sweep(r, carry):
        p0 = px[r + 1]
        w_below = wv_v[r]
        w_above = pltpu.roll(w_below, 1, 0)
        acc = base_v[r] + wr_v[r] * from_right(p0, right_edge(pack2_r[1], r)) + wl_v[r] * from_left(p0, left_edge(pack2_r[0], r))
        acc += wu_v[r] * px[r] + wu_v[r + 1] * px[r + 2]
        acc += w_below * pltpu.roll(p0, layers - 1, 0) + w_above * pltpu.roll(p0, 1, 0)
        qx[r] = acc * inv_v[r]
        pltpu.make_async_copy(qx.at[r], new_head.at[:, r, :], out_sem.at[0]).start()
        return carry

    lax.fori_loop(0, rows, second_sweep, 0)
    for c in sent:
        c.wait_send()
    for c in gather:
        c.wait_send()
    gather[0].wait_recv()
    for c in relays:
        c.wait()
    pltpu.make_async_copy(qx, qx, out_sem.at[0]).wait()


def body(head, conductivity, root_layer, veg_type, uptake_rate, depth, conveyance, elevation, land_mask):
    layers, rows, cols = head.shape
    ncol = lax.axis_size("gy") * lax.axis_size("ga")
    near = ncol // 2 - 1
    f32 = jnp.float32
    slab = (rows, layers, cols)
    ext = (rows + 2, layers, cols)
    hbm = pl.BlockSpec(memory_space=pl.ANY)
    window = (rows + 2 * RING, cols + EDGE)
    return pl.pallas_call(
        kernel,
        out_shape=(pltpu.VMEM(head.shape, f32), pltpu.VMEM(depth.shape, f32)),
        in_specs=[hbm] * 4 + [pl.BlockSpec(memory_space=pltpu.SMEM)] + [hbm] * 4,
        out_specs=(pl.BlockSpec(memory_space=pltpu.VMEM),) * 2,
        scratch_shapes=[
            pltpu.VMEM(ext, f32),
            pltpu.VMEM(ext, f32),
            pltpu.VMEM(ext, f32),
            pltpu.VMEM(slab, f32),
            pltpu.VMEM((rows, cols), jnp.int32),
            pltpu.VMEM((rows, cols), jnp.int32),
            pltpu.VMEM((3,) + window, f32),
            pltpu.VMEM(window, jnp.int32),
            pltpu.VMEM(window, f32),
            pltpu.VMEM((2, rows, cols), f32),
            pltpu.VMEM((rows, cols), f32),
            pltpu.VMEM(slab, f32),
            pltpu.VMEM(slab, f32),
            pltpu.VMEM((rows + 1, layers, cols), f32),
            pltpu.VMEM(slab, f32),
            pltpu.VMEM(slab, f32),
            pltpu.VMEM(slab, f32),
            pltpu.VMEM((2, layers, LANES), f32),
            pltpu.VMEM((2, layers, LANES), f32),
            pltpu.VMEM((2, layers, LANES), f32),
            pltpu.VMEM((2, layers, LANES), f32),
            pltpu.SemaphoreType.DMA((17,)),
            pltpu.SemaphoreType.DMA((22,)),
            pltpu.SemaphoreType.DMA((22,)),
            pltpu.SemaphoreType.DMA((near + 1,)),
            pltpu.SemaphoreType.DMA((near + 1,)),
            pltpu.SemaphoreType.DMA((near,)),
            pltpu.SemaphoreType.DMA((near,)),
            pltpu.SemaphoreType.DMA((1,)),
        ],
        compiler_params=pltpu.CompilerParams(collective_id=0, has_side_effects=True),
        name="watershed_step",
    )(head, conductivity, root_layer, veg_type, uptake_rate, depth, conveyance, elevation, land_mask)


def solution(mesh):
    return jax.shard_map(
        body,
        mesh=mesh,
        in_specs=(
            P(None, "gx", ("gy", "ga")),
            P(None, "gx", ("gy", "ga")),
            P("gx", ("gy", "ga")),
            P("gx", ("gy", "ga")),
            P(),
            P("gx", None),
            P("gx", None),
            P("gx", None),
            P("gx", None),
        ),
        out_specs=(P(None, "gx", ("gy", "ga")), P("gx", None)),
        check_vma=False,
    )
```

```python
import functools

import jax
import jax.numpy as jnp
from jax import lax
from jax.experimental import pallas as pl
from jax.experimental.pallas import tpu as pltpu
from jax.sharding import PartitionSpec as P

NVEG = 17
SSW = 4
RING = 4
LANES = 128
EDGE = 2 * LANES

exchange_coef = 0.5
storage_coef = 0.5
MESH = pl.DeviceIdType.MESH


def harmonic(first, second):
    total = first + second
    return 2.0 * first * second / jnp.where(total > 0, total, 1.0)


def lane_of(shape):
    return lax.broadcasted_iota(jnp.int32, shape, len(shape) - 1)


def row_of(shape):
    return lax.broadcasted_iota(jnp.int32, shape, len(shape) - 2)


def from_right(x, edge):
    width = x.shape[1]
    y = pltpu.roll(x, width - 1, 1)
    tail = jnp.where(lane_of(edge.shape) == LANES - 1, edge, y[:, width - LANES :])
    return jnp.concatenate([y[:, : width - LANES], tail], axis=1)


def from_left(x, edge):
    y = pltpu.roll(x, 1, 1)
    front = jnp.where(lane_of(edge.shape) == 0, edge, y[:, :LANES])
    return jnp.concatenate([front, y[:, LANES:]], axis=1)


def circular(window, cols):
    left = window[:, :LANES]
    right = window[:, cols + LANES :]
    side = jnp.where(lane_of(left.shape) < LANES // 2, right, left)
    return jnp.concatenate([window[:, LANES : cols + LANES], side], axis=1)


def kernel(
    head, cond, root, veg, uptake, depth, conv, elev, mask,
    new_head, new_depth,
    hx, cx, px, qx, root_v, veg_v, field, mask_v, top_v, cpl_v, sink_v,
    wr_v, wl_v, wu_v, wv_v, inv_v, base_v,
    pack_s, pack_r, pack2_s, pack2_r,
    load_sem, send_sem, recv_sem, gsend_sem, grecv_sem, rsend_sem, rrecv_sem, out_sem,
):
    layers, rows, cols = head.shape
    gx = lax.axis_index("gx")
    gy = lax.axis_index("gy")
    ga = lax.axis_index("ga")
    ngx = lax.axis_size("gx")
    nga = lax.axis_size("ga")
    ncol = lax.axis_size("gy") * nga
    col = gy * nga + ga
    off = pl.multiple_of(col * cols, LANES)
    total = ncol * cols

    def at(dx, dc):
        c = lax.rem(col + dc + ncol, ncol)
        return (lax.rem(gx + dx + ngx, ngx), c // nga, lax.rem(c, nga))

    ngy = lax.axis_size("gy")

    def same_core(dy, dz):
        return (gx, lax.rem(gy + 2 * dy + ngy, ngy), lax.rem(ga + dz + nga, nga))

    def block_cols(device):
        return pl.ds(pl.multiple_of((device[1] * nga + device[2]) * cols, LANES), cols)

    chips = sorted(
        ((dy, dz) for dy in range(ngy // 2) for dz in range(nga) if (dy, dz) != (0, 0)),
        key=lambda v: min(v[0], ngy // 2 - v[0]) + v[1],
    )
    partner = (gx, gy + 1 - 2 * lax.rem(gy, 2), ga)
    barrier = pltpu.get_barrier_semaphore()
    up, down = gx > 0, gx < ngx - 1
    left, right = col > 0, col < ncol - 1
    ways = {
        (1, 0): (at(1, 0), down, up),
        (-1, 0): (at(-1, 0), up, down),
        (0, 1): (at(0, 1), right, left),
        (0, -1): (at(0, -1), left, right),
        (1, 1): (at(1, 1), down & right, up & left),
        (1, -1): (at(1, -1), down & left, up & right),
        (-1, 1): (at(-1, 1), up & right, down & left),
        (-1, -1): (at(-1, -1), up & left, down & right),
    }

    def greet(device):
        pl.semaphore_signal(barrier, inc=1, device_id=device, device_id_type=MESH)

    for device, there, _ in ways.values():
        pl.when(there)(functools.partial(greet, device))
    always = [partner] + [same_core(*v) for v in chips]
    for device in always:
        greet(device)
    present = [there.astype(jnp.int32) for _, there, _ in ways.values()]
    n_peers = functools.reduce(lambda p, q: p + q, present) + len(always)

    left_off = pl.multiple_of(lax.rem(off - LANES + total, total), LANES)
    right_off = pl.multiple_of(lax.rem(off + cols, total), LANES)
    loads = []
    for n, src in enumerate((depth, conv, elev)):
        loads.append(pltpu.make_async_copy(src.at[:, pl.ds(left_off, LANES)], field.at[n, 0:rows, 0:LANES], load_sem.at[3 * n]))
        loads.append(pltpu.make_async_copy(src.at[:, pl.ds(off, cols)], field.at[n, 0:rows, LANES : LANES + cols], load_sem.at[3 * n + 1]))
        loads.append(pltpu.make_async_copy(src.at[:, pl.ds(right_off, LANES)], field.at[n, 0:rows, LANES + cols :], load_sem.at[3 * n + 2]))
    loads.append(pltpu.make_async_copy(mask.at[:, pl.ds(left_off, LANES)], mask_v.at[0:rows, 0:LANES], load_sem.at[9]))
    loads.append(pltpu.make_async_copy(mask.at[:, pl.ds(off, cols)], mask_v.at[0:rows, LANES : LANES + cols], load_sem.at[10]))
    loads.append(pltpu.make_async_copy(mask.at[:, pl.ds(right_off, LANES)], mask_v.at[0:rows, LANES + cols :], load_sem.at[11]))
    loads.append(pltpu.make_async_copy(head.at[0], top_v.at[0:rows, LANES : LANES + cols], load_sem.at[12]))
    loads.append(pltpu.make_async_copy(root, root_v, load_sem.at[13]))
    loads.append(pltpu.make_async_copy(veg, veg_v, load_sem.at[14]))
    for c in loads:
        c.start()
    for r in range(rows):
        pltpu.make_async_copy(head.at[:, r, :], hx.at[r + 1], load_sem.at[15]).start()
        pltpu.make_async_copy(cond.at[:, r, :], cx.at[r + 1], load_sem.at[16]).start()

    def blank(*refs):
        for ref in refs:
            ref[...] = jnp.zeros(ref.shape, ref.dtype)

    low_rows = pl.ds(rows, RING)
    high_rows = pl.ds(rows + RING, RING)
    tall = rows + 2 * RING

    @pl.when(gx == 0)
    def _():
        blank(hx.at[0], cx.at[0], px.at[0], top_v.at[high_rows], mask_v.at[high_rows])
        field[:, rows + RING : tall, :] = jnp.zeros((3, RING, cols + EDGE), jnp.float32)

    @pl.when(gx == ngx - 1)
    def _():
        blank(hx.at[rows + 1], cx.at[rows + 1], px.at[rows + 1], top_v.at[low_rows], mask_v.at[low_rows])
        field[:, rows : rows + RING, :] = jnp.zeros((3, RING, cols + EDGE), jnp.float32)

    @pl.when(col == 0)
    def _():
        blank(pack_r.at[0], pack2_r.at[0], top_v.at[:, pl.ds(0, LANES)])

    @pl.when(col == ncol - 1)
    def _():
        blank(pack_r.at[1], pack2_r.at[1], top_v.at[:, pl.ds(LANES + cols, LANES)])

    for c in loads:
        c.wait()
    pl.semaphore_wait(barrier, n_peers)

    sent = []
    count = [0]

    def send(way, *pairs):
        device, there, from_there = ways[way]
        copies = []
        for src, dst in pairs:
            n = count[0]
            count[0] += 1
            copies.append(
                pltpu.make_async_remote_copy(
                    src_ref=src, dst_ref=dst, send_sem=send_sem.at[n], recv_sem=recv_sem.at[n],
                    device_id=device, device_id_type=MESH,
                )
            )

        @pl.when(there)
        def _():
            for c in copies:
                c.start()

        sent.append((there, from_there, copies))
        return sent[-1]

    def arrived(groups):
        for _, from_there, copies in groups:

            @pl.when(from_there)
            def _():
                for c in copies:
                    c.wait_recv()

    def gone(groups):
        for there, _, copies in groups:

            @pl.when(there)
            def _():
                for c in copies:
                    c.wait_send()

    lo = pl.ds(rows, RING)
    hi = pl.ds(rows + RING, RING)
    first = pl.ds(0, RING)
    last = pl.ds(rows - RING, RING)
    own = pl.ds(LANES, cols)
    lt = pl.ds(0, LANES)
    rt = pl.ds(LANES + cols, LANES)
    hl = pl.ds(0, LANES)
    hr = pl.ds(cols - LANES, LANES)
    every = pl.ds(0, rows)
    surface = [
        send(
            (1, 0),
            (field.at[:, last, :], field.at[:, hi, :]),
            (mask_v.at[last, :], mask_v.at[hi, :]),
            (head.at[0, last, :], top_v.at[hi, own]),
        ),
        send(
            (-1, 0),
            (field.at[:, first, :], field.at[:, lo, :]),
            (mask_v.at[first, :], mask_v.at[lo, :]),
            (head.at[0, first, :], top_v.at[lo, own]),
        ),
        send((1, 1), (head.at[0, last, hr], top_v.at[hi, lt])),
        send((1, -1), (head.at[0, last, hl], top_v.at[hi, rt])),
        send((-1, 1), (head.at[0, first, hr], top_v.at[lo, lt])),
        send((-1, -1), (head.at[0, first, hl], top_v.at[lo, rt])),
        send((0, 1), (head.at[0, :, hr], top_v.at[every, lt])),
        send((0, -1), (head.at[0, :, hl], top_v.at[every, rt])),
    ]
    soil = [
        send(
            (1, 0),
            (head.at[:, rows - 1, :], hx.at[0]),
            (cond.at[:, rows - 1, :], cx.at[0]),
        ),
        send(
            (-1, 0),
            (head.at[:, 0, :], hx.at[rows + 1]),
            (cond.at[:, 0, :], cx.at[rows + 1]),
        ),
    ]

    def surface_block(high, outside):
        wide = cols + LANES
        dep = circular(field[0, 0:high, :], cols)
        con = circular(field[1, 0:high, :], cols)
        bed = circular(field[2, 0:high, :], cols)
        cpl = exchange_coef * circular(mask_v[0:high, :], cols).astype(jnp.float32)
        top = circular(top_v[0:high, :], cols)
        drag = con * jnp.exp(jnp.log(dep) * (5.0 / 3.0))
        lane = lane_of((high, wide))
        outside |= (lane >= cols) & (lane < cols + LANES // 2) & (col == ncol - 1)
        outside |= (lane >= cols + LANES // 2) & (col == 0)
        drag = jnp.where(outside, 0.0, drag)
        w_r = harmonic(drag, pltpu.roll(drag, wide - 1, 1))
        w_l = pltpu.roll(w_r, 1, 1)
        w_d = harmonic(drag, pltpu.roll(drag, high - 1, 0))
        w_u = pltpu.roll(w_d, 1, 0)
        wsum = (w_r + w_l) + (w_d + w_u)
        inv = 1.0 / (1.0 + cpl + wsum)
        part = (dep + cpl * top - wsum * bed) * inv
        w_r = w_r * inv
        w_l = w_l * inv
        w_d = w_d * inv
        w_u = w_u * inv
        level = dep
        for _ in range(SSW):
            t = level + bed
            level = part + (
                (w_r * pltpu.roll(t, wide - 1, 1) + w_l * pltpu.roll(t, 1, 1))
                + (w_d * pltpu.roll(t, high - 1, 0) + w_u * pltpu.roll(t, 1, 0))
            )
        return level, cpl

    def spread():
        mine = block_cols((gx, gy, ga))
        out = []
        for n, device in enumerate([partner] + [same_core(*v) for v in chips]):
            c = pltpu.make_async_remote_copy(
                src_ref=new_depth.at[:, mine], dst_ref=new_depth.at[:, mine],
                send_sem=gsend_sem.at[n], recv_sem=grecv_sem.at[n],
                device_id=device, device_id_type=MESH,
            )
            c.start()
            out.append(c)
        return out

    def relay(n):
        dy, dz = chips[n]
        theirs = block_cols(same_core(-dy, -dz))
        c = pltpu.make_async_remote_copy(
            src_ref=new_depth.at[:, theirs], dst_ref=new_depth.at[:, theirs],
            send_sem=rsend_sem.at[n], recv_sem=rrecv_sem.at[n],
            device_id=partner, device_id_type=MESH,
        )
        c.start()
        return c

    pltpu.make_async_copy(hx.at[pl.ds(1, rows)], hx.at[pl.ds(1, rows)], load_sem.at[15]).wait()
    pltpu.make_async_copy(cx.at[pl.ds(1, rows)], cx.at[pl.ds(1, rows)], load_sem.at[16]).wait()

    def pack(fields, out):
        to_right = jnp.zeros((layers, LANES), jnp.float32)
        to_left = jnp.zeros((layers, LANES), jnp.float32)
        lane = lane_of((layers, LANES))
        for n, ref in enumerate(fields):
            for r in range(rows):
                slot = n * rows + r
                tail = pltpu.roll(ref[r + 1, :, cols - LANES : cols], (slot + 1) % LANES, 1)
                to_right = jnp.where(lane == slot, tail, to_right)
                front = ref[r + 1, :, 0:LANES]
                front = pltpu.roll(front, slot, 1) if slot else front
                to_left = jnp.where(lane == slot, front, to_left)
        out[0] = to_right
        out[1] = to_left

    pack((hx, cx), pack_s)
    soil += [
        send((0, 1), (pack_s.at[0], pack_r.at[0])),
        send((0, -1), (pack_s.at[1], pack_r.at[1])),
    ]

    rate = jnp.zeros((rows, cols), jnp.float32)
    kinds = veg_v[...]
    for k in range(NVEG):
        rate = jnp.where(kinds == k, uptake[k], rate)
    sink_v[...] = rate / (root_v[...].astype(jnp.float32) + 1.0)

    arrived(surface)
    high = rows + 2 * RING
    rowi = row_of((high, cols + LANES))
    outside = (rowi >= rows) & (rowi < rows + RING) & (gx == ngx - 1)
    outside |= (rowi >= rows + RING) & (gx == 0)
    level, cpl = surface_block(high, outside)
    block = level[0:rows, 0:cols]
    new_depth[:, block_cols((gx, gy, ga))] = block
    gather = spread()
    coupling = cpl[0:rows, 0:cols]
    cpl_v[0] = coupling
    cpl_v[1] = coupling * block

    arrived(soil)
    has_up = jnp.where(gx > 0, 1.0, 0.0)
    has_down = jnp.where(gx < ngx - 1, 1.0, 0.0)
    has_left = jnp.where(col > 0, 1.0, 0.0)
    has_right = jnp.where(col < ncol - 1, 1.0, 0.0)
    layer = row_of((layers, cols))
    lane0 = lane_of((layers, LANES)) == 0

    def right_edge(packed, slot):
        return pltpu.roll(packed, lax.rem(2 * LANES - 1 - slot, LANES), 1)

    def left_edge(packed, slot):
        return pltpu.roll(packed, lax.rem(2 * LANES - slot, LANES), 1)

    def first_sweep(r, w_up):
        c0 = cx[r + 1]
        h0 = hx[r + 1]
        w_down = harmonic(c0, cx[r + 2]) * jnp.where(r == rows - 1, has_down, 1.0)
        edge_r = right_edge(pack_r[1], rows + r) * has_right
        edge_l = left_edge(pack_r[0], rows + r) * has_left
        w_right = harmonic(c0, from_right(c0, edge_r))
        w_left = from_left(w_right, harmonic(c0[:, :LANES], edge_l))
        w_below = jnp.where(layer == layers - 1, 0.0, harmonic(c0, pltpu.roll(c0, layers - 1, 0)))
        w_above = pltpu.roll(w_below, 1, 0)
        on_top = layer == 0
        coupled = jnp.where(on_top, cpl_v[0, pl.ds(r, 1), :], 0.0)
        source = jnp.where(on_top, cpl_v[1, pl.ds(r, 1), :], 0.0)
        uptake_here = jnp.where(layer <= root_v[pl.ds(r, 1), :], sink_v[pl.ds(r, 1), :], 0.0)
        inv_here = 1.0 / (
            (storage_coef + coupled) + ((w_right + w_left) + (w_up + w_down)) + (w_below + w_above)
        )
        base = (storage_coef * h0 - uptake_here + source) + (w_above - w_below)
        wr_v[r] = w_right
        wl_v[r] = w_left
        wu_v[r] = w_up
        wv_v[r] = w_below
        inv_v[r] = inv_here
        base_v[r] = base
        acc = base + w_right * from_right(h0, right_edge(pack_r[1], r)) + w_left * from_left(h0, left_edge(pack_r[0], r))
        acc += w_up * hx[r] + w_down * hx[r + 2]
        acc += w_below * pltpu.roll(h0, layers - 1, 0) + w_above * pltpu.roll(h0, 1, 0)
        px[r + 1] = acc * inv_here
        return w_down

    wu_v[rows] = lax.fori_loop(0, rows, first_sweep, harmonic(cx[0], cx[1]) * has_up)

    second = [
        send((1, 0), (px.at[rows], px.at[0])),
        send((-1, 0), (px.at[1], px.at[rows + 1])),
    ]
    pack((px,), pack2_s)
    second += [
        send((0, 1), (pack2_s.at[0], pack2_r.at[0])),
        send((0, -1), (pack2_s.at[1], pack2_r.at[1])),
    ]
    relays = []
    for n in range(len(chips)):
        gather[n + 1].wait_recv()
        relays.append(relay(n))
    arrived(second)

    def second_sweep(r, carry):
        p0 = px[r + 1]
        w_below = wv_v[r]
        w_above = pltpu.roll(w_below, 1, 0)
        acc = base_v[r] + wr_v[r] * from_right(p0, right_edge(pack2_r[1], r)) + wl_v[r] * from_left(p0, left_edge(pack2_r[0], r))
        acc += wu_v[r] * px[r] + wu_v[r + 1] * px[r + 2]
        acc += w_below * pltpu.roll(p0, layers - 1, 0) + w_above * pltpu.roll(p0, 1, 0)
        qx[r] = acc * inv_v[r]
        pltpu.make_async_copy(qx.at[r], new_head.at[:, r, :], out_sem.at[0]).start()
        return carry

    lax.fori_loop(0, rows, second_sweep, 0)
    gone(sent)
    for c in gather:
        c.wait_send()
    gather[0].wait_recv()
    for c in relays:
        c.wait()
    pltpu.make_async_copy(qx, qx, out_sem.at[0]).wait()


def body(head, conductivity, root_layer, veg_type, uptake_rate, depth, conveyance, elevation, land_mask):
    layers, rows, cols = head.shape
    ncol = lax.axis_size("gy") * lax.axis_size("ga")
    near = ncol // 2 - 1
    f32 = jnp.float32
    slab = (rows, layers, cols)
    ext = (rows + 2, layers, cols)
    hbm = pl.BlockSpec(memory_space=pl.ANY)
    window = (rows + 2 * RING, cols + EDGE)
    return pl.pallas_call(
        kernel,
        out_shape=(pltpu.VMEM(head.shape, f32), pltpu.VMEM(depth.shape, f32)),
        in_specs=[hbm] * 4 + [pl.BlockSpec(memory_space=pltpu.SMEM)] + [hbm] * 4,
        out_specs=(pl.BlockSpec(memory_space=pltpu.VMEM),) * 2,
        scratch_shapes=[
            pltpu.VMEM(ext, f32),
            pltpu.VMEM(ext, f32),
            pltpu.VMEM(ext, f32),
            pltpu.VMEM(slab, f32),
            pltpu.VMEM((rows, cols), jnp.int32),
            pltpu.VMEM((rows, cols), jnp.int32),
            pltpu.VMEM((3,) + window, f32),
            pltpu.VMEM(window, jnp.int32),
            pltpu.VMEM(window, f32),
            pltpu.VMEM((2, rows, cols), f32),
            pltpu.VMEM((rows, cols), f32),
            pltpu.VMEM(slab, f32),
            pltpu.VMEM(slab, f32),
            pltpu.VMEM((rows + 1, layers, cols), f32),
            pltpu.VMEM(slab, f32),
            pltpu.VMEM(slab, f32),
            pltpu.VMEM(slab, f32),
            pltpu.VMEM((2, layers, LANES), f32),
            pltpu.VMEM((2, layers, LANES), f32),
            pltpu.VMEM((2, layers, LANES), f32),
            pltpu.VMEM((2, layers, LANES), f32),
            pltpu.SemaphoreType.DMA((17,)),
            pltpu.SemaphoreType.DMA((22,)),
            pltpu.SemaphoreType.DMA((22,)),
            pltpu.SemaphoreType.DMA((near + 1,)),
            pltpu.SemaphoreType.DMA((near + 1,)),
            pltpu.SemaphoreType.DMA((near,)),
            pltpu.SemaphoreType.DMA((near,)),
            pltpu.SemaphoreType.DMA((1,)),
        ],
        compiler_params=pltpu.CompilerParams(collective_id=0, has_side_effects=True),
        name="watershed_step",
    )(head, conductivity, root_layer, veg_type, uptake_rate, depth, conveyance, elevation, land_mask)


def solution(mesh):
    return jax.shard_map(
        body,
        mesh=mesh,
        in_specs=(
            P(None, "gx", ("gy", "ga")),
            P(None, "gx", ("gy", "ga")),
            P("gx", ("gy", "ga")),
            P("gx", ("gy", "ga")),
            P(),
            P("gx", None),
            P("gx", None),
            P("gx", None),
            P("gx", None),
        ),
        out_specs=(P(None, "gx", ("gy", "ga")), P("gx", None)),
        check_vma=False,
    )
```
